32 devices in a mesh: seq: 16 (over z, y, x), head: 2 (over core).
Axes of the slice: x: 2, y: 2, z: 4, core: 2. Of those that a mesh axis runs over, the one named last changes fastest.
Arguments:
- queries: bfloat16 [6144, 3072], P('seq', 'head'), may hold values from -6 to 6
- keys: bfloat16 [6144, 3072], P('seq', 'head'), may hold values from -6 to 6
- values: bfloat16 [6144, 3072], P('seq', 'head'), may hold values from -6 to 6
- text_keys: bfloat16 [512, 3072], P('seq', 'head'), may hold values from -6 to 6
- text_values: bfloat16 [512, 3072], P('seq', 'head'), may hold values from -6 to 6
- neighbours: int32 [16, 5], P('seq'), may hold values from -1 to 15, as said below
- clip_lengths: int32 [4], replicated, may hold values from 1 to 7, as said below
- text_lengths: int32 [4], replicated, may hold values from 1 to 224, as said below
- out_weight: bfloat16 [3072, 3072], P('head'), may hold values from -0.109375 to 0.109375
Outputs:
- mixed: bfloat16 [6144, 3072], P(('seq', 'head'))
The draws below stay inside these ranges and needn't reach their ends.
Inputs may be any that keep to these rules, and one draw needn't show every extreme that they name: Clips lie end to end and fill all 16 tiles; each clip is laid out in frames of 1 to 3 tiles, and a tile lists itself, its neighbours within its frame and the tiles at the same place in the frames before and after, all inside its clip. `clip_lengths`: the lengths sum to 16. `text_lengths`: A clip's text length is at most its tiles times 32; every clip of 7 tiles fills all its text slots, and every clip of one tile has one text token.
All inputs are finite; a program needn't handle non-finite values.
Results may differ from the reference program's by a relative error of at most 0.012.
Values may be sent and summed in bfloat16 or wider, within the bound.
A program may use at most 192 MiB of HBM per device.

```python
import jax
import jax.numpy as jnp
from jax import lax

D = 3072
HEADS = 24
HD = 128
TILE = 384
TXT_DEV = 32
REACH = 3
MOST = 7
CLIPS = 4
TOKENS = 6144
TEXT = 512
N_SEQ = 16
N_HEAD = 2


def clip_plan(key):
    base = jax.random.fold_in(key, 11)
    first, second, third, fourth = jax.random.split(base, 4)
    spread = jax.random.randint(first, (CLIPS // 2,), 0, 4).at[0].set(3)
    lengths = jnp.stack([4 + spread, 4 - spread], axis=1).reshape(CLIPS)
    order = jax.random.permutation(fourth, CLIPS)
    lengths = lengths[order].astype(jnp.int32)
    frames = jax.random.randint(second, (CLIPS,), 1, REACH + 1).astype(jnp.int32)
    text = jax.random.randint(third, (CLIPS,), 1, lengths * TXT_DEV + 1).astype(jnp.int32)
    text = jnp.where(lengths == MOST, lengths * TXT_DEV, text)
    text = jnp.where(lengths == 1, 1, text).astype(jnp.int32)
    starts = jnp.cumsum(lengths) - lengths
    tiles = jnp.arange(N_SEQ, dtype=jnp.int32)
    clip_of = jnp.sum((tiles[:, None] >= starts[None, :]).astype(jnp.int32), axis=1) - 1
    inner = tiles - starts[clip_of]
    width = frames[clip_of]
    count = lengths[clip_of]
    empty = jnp.full_like(tiles, -1)
    left = jnp.where(inner % width != 0, tiles - 1, empty)
    right = jnp.where(((inner + 1) % width != 0) & (inner + 1 < count), tiles + 1, empty)
    before = jnp.where(inner >= width, tiles - width, empty)
    after = jnp.where(inner + width < count, tiles + width, empty)
    listed = jnp.stack([tiles, left, right, before, after], axis=1).astype(jnp.int32)
    return (lengths, text, listed)


def draw_neighbours(key, part):
    return clip_plan(key)[2]


def draw_clip_lengths(key, part):
    return clip_plan(key)[0]


def draw_text_lengths(key, part):
    return clip_plan(key)[1]


def draw_queries(key, part):
    noise = jnp.clip(jax.random.normal(jax.random.fold_in(key, 31), (TOKENS, HEADS * HD), jnp.float32), -6.0, 6.0)
    return noise.astype(jnp.bfloat16)


def draw_keys(key, part):
    noise = jnp.clip(jax.random.normal(jax.random.fold_in(key, 37), (TOKENS, HEADS * HD), jnp.float32), -6.0, 6.0)
    return noise.astype(jnp.bfloat16)


def levels(rng, shape, cuts, low, largest):
    def one(dim, blocks):
        steps = jax.random.uniform(jax.random.fold_in(jax.random.fold_in(rng, 6), dim), (blocks,), jnp.float32, low / len(cuts), largest / len(cuts))
        return jnp.repeat(jnp.exp(steps), shape[dim] // blocks).reshape((-1,) + (1,) * (len(shape) - dim - 1))

    level = one(*cuts[0])
    for cut in cuts[1:]:
        level = level * one(*cut)
    return level


def normal_values(own_key, shape, deviation, most, cuts=(), held_as=jnp.bfloat16):
    array = jax.random.normal(own_key, shape, jnp.float32) * deviation
    if len(cuts) > 0:
        array = levels(own_key, shape, cuts, -0.22, 0.18) * array
    return jnp.clip(array, min=-most, max=most).astype(held_as)


def setup_inputs(seed: int = 0) -> dict:
    key_list = jax.random.split(jax.random.key(seed), 10)
    queries = draw_queries(jax.random.fold_in(key_list[9], 71), 0)
    keys = draw_keys(jax.random.fold_in(key_list[9], 71), 0)
    values = normal_values(key_list[2], (TOKENS, HEADS * HD), 1.0, 6.0, ((0, 16), (1, 2)))
    text_keys = normal_values(key_list[3], (TEXT, HEADS * HD), 1.0, 6.0, ((0, 16), (1, 2)))
    text_values = normal_values(key_list[4], (TEXT, HEADS * HD), 1.0, 6.0, ((0, 16), (1, 2)))
    neighbours = draw_neighbours(jax.random.fold_in(key_list[9], 71), 0)
    clip_lengths = draw_clip_lengths(jax.random.fold_in(key_list[9], 71), 0)
    text_lengths = draw_text_lengths(jax.random.fold_in(key_list[9], 71), 0)
    out_weight = normal_values(key_list[8], (HEADS * HD, D), (HEADS * HD) ** -0.5, 0.109375, ((0, 2),))
    return {"queries": queries, "keys": keys, "values": values, "text_keys": text_keys, "text_values": text_values, "neighbours": neighbours, "clip_lengths": clip_lengths, "text_lengths": text_lengths, "out_weight": out_weight}


def reference(queries, keys, values, text_keys, text_values, neighbours, clip_lengths, text_lengths, out_weight):
    starts = jnp.cumsum(clip_lengths) - clip_lengths
    tiles = jnp.arange(N_SEQ, dtype=jnp.int32)
    clip_of = (jnp.sum((tiles[:, None] >= starts[None, :]).astype(jnp.int32), axis=1) - 1).astype(jnp.int32)
    text_low = starts[clip_of] * TXT_DEV
    text_high = text_low + text_lengths[clip_of]
    span = 2 * REACH + 1
    text_span = 2 * MOST - 1
    key_pad = jnp.pad(keys, ((REACH * TILE, REACH * TILE), (0, 0)))
    value_pad = jnp.pad(values, ((REACH * TILE, REACH * TILE), (0, 0)))
    tkey_pad = jnp.pad(text_keys, (((MOST - 1) * TXT_DEV, (MOST - 1) * TXT_DEV), (0, 0)))
    tvalue_pad = jnp.pad(text_values, (((MOST - 1) * TXT_DEV, (MOST - 1) * TXT_DEV), (0, 0)))
    scale = HD ** -0.5

    def one_tile(tile):
        tile = tile.astype(jnp.int32)
        q_rows = lax.dynamic_slice_in_dim(queries, tile * TILE, TILE, 0)
        k_rows = lax.dynamic_slice_in_dim(key_pad, tile * TILE, span * TILE, 0)
        v_rows = lax.dynamic_slice_in_dim(value_pad, tile * TILE, span * TILE, 0)
        offsets = jnp.arange(span, dtype=jnp.int32) - REACH
        listed = neighbours[tile]
        present = jnp.any((listed[None, :] == (tile + offsets)[:, None]) & (listed[None, :] >= 0), axis=1)
        tile_mask = jnp.repeat(present, TILE)
        tk_rows = lax.dynamic_slice_in_dim(tkey_pad, tile * TXT_DEV, text_span * TXT_DEV, 0)
        tv_rows = lax.dynamic_slice_in_dim(tvalue_pad, tile * TXT_DEV, text_span * TXT_DEV, 0)
        global_rows = tile * TXT_DEV - (MOST - 1) * TXT_DEV + jnp.arange(text_span * TXT_DEV, dtype=jnp.int32)
        text_mask = (global_rows >= text_low[tile]) & (global_rows < text_high[tile])
        all_keys = jnp.concatenate([k_rows, tk_rows], axis=0)
        all_values = jnp.concatenate([v_rows, tv_rows], axis=0)
        mask = jnp.concatenate([tile_mask, text_mask], axis=0)
        qf = q_rows.reshape(TILE, HEADS, HD).astype(jnp.float32)
        kf = all_keys.reshape(-1, HEADS, HD).astype(jnp.float32)
        vf = all_values.reshape(-1, HEADS, HD).astype(jnp.float32)
        score = jnp.einsum("qhd,khd->hqk", qf, kf) * scale
        score = jnp.where(mask[None, None, :], score, -1e30)
        top = jnp.max(score, axis=-1)
        weight = jnp.where(mask[None, None, :], jnp.exp(score - top[..., None]), 0.0)
        total = jnp.sum(weight, axis=-1)
        rounded = lax.optimization_barrier(weight.astype(jnp.bfloat16))
        acc = jnp.einsum("hqk,khd->hqd", rounded.astype(jnp.float32), vf)
        attended = acc / total[..., None]
        return jnp.transpose(attended, (1, 0, 2)).reshape(TILE, HEADS * HD).astype(jnp.bfloat16)

    attended = lax.map(one_tile, tiles).reshape(N_SEQ * TILE, HEADS * HD)
    group = HEADS * HD // N_HEAD
    parts = attended.reshape(N_SEQ * TILE, N_HEAD, group)
    weights = out_weight.reshape(N_HEAD, group, D)

    def add_group(total, index):
        piece = jnp.dot(parts[:, index, :], weights[index], preferred_element_type=jnp.float32)
        rounded = lax.optimization_barrier(piece.astype(jnp.bfloat16))
        return total + rounded.astype(jnp.float32), None

    summed, unused = lax.scan(add_group, jnp.zeros((N_SEQ * TILE, D), jnp.float32), jnp.arange(N_HEAD, dtype=jnp.int32))
    return summed.astype(jnp.bfloat16)
```

```python
import functools

import jax
import jax.numpy as jnp
from jax import lax
from jax.experimental import pallas as pl
from jax.experimental.pallas import tpu as pltpu
from jax.sharding import PartitionSpec as P

HD = 128
MOST = 7
SPAN = 2 * MOST - 1
GROUP = 3
LOW = -1e30
MESH = pl.DeviceIdType.MESH


def kernel(
    n_seq,
    n_head,
    near_ref,
    clip_ref,
    text_ref,
    q_hbm,
    k_hbm,
    v_hbm,
    tk_hbm,
    tv_hbm,
    w_hbm,
    out_ref,
    q,
    kv,
    text,
    stage,
    w,
    acc,
    top,
    total,
    attended,
    partial,
    arrived,
    near_send,
    near_recv,
    far_send,
    far_recv,
    text_send,
    text_recv,
    out_send,
    out_recv,
    local_sem,
):
    me = lax.axis_index("seq")
    head = lax.axis_index("head")
    rows, width = q.shape
    heads = width // HD
    group = GROUP if heads % GROUP == 0 else 1
    chunks = heads // group
    cw = group * HD
    trows = tk_hbm.shape[0]
    text_pad = text.shape[1]

    def exists(by):
        return (me + by >= 0) & (me + by < n_seq)

    def near_slot(by):
        return 1 if by == 1 else 2

    def far_slot(by):
        return 3 if by == 2 else 4

    own_copies = [
        pltpu.make_async_copy(q_hbm, q, local_sem.at[0]),
        pltpu.make_async_copy(k_hbm, kv.at[0, pl.ds(0, rows)], local_sem.at[1]),
        pltpu.make_async_copy(v_hbm, kv.at[1, pl.ds(0, rows)], local_sem.at[2]),
        pltpu.make_async_copy(tk_hbm, text.at[0, pl.ds((MOST - 1) * trows, trows)], local_sem.at[3]),
        pltpu.make_async_copy(tv_hbm, text.at[1, pl.ds((MOST - 1) * trows, trows)], local_sem.at[4]),
    ]
    w_copy = pltpu.make_async_copy(w_hbm, w, local_sem.at[5])
    text[...] = jnp.zeros_like(text)
    for copy in own_copies:
        copy.start()
    w_copy.start()
    for by in (1, -1):
        for slot, step in ((near_slot(by), by), (far_slot(by * 2), by * 2)):

            @pl.when(jnp.logical_not(exists(-step)))
            def _():
                kv[:, pl.ds(slot * rows, rows), :] = jnp.zeros((2, rows, width), kv.dtype)

    barrier = pltpu.get_barrier_semaphore()
    partners = n_head - 1
    for by in (1, -1, 2, -2):
        partners = partners + exists(by).astype(jnp.int32)

        @pl.when(exists(by))
        def _():
            pl.semaphore_signal(barrier, inc=1, device_id={"seq": me + by}, device_id_type=MESH)

    for d in range(1, n_head):
        pl.semaphore_signal(
            barrier, inc=1, device_id={"head": lax.rem(head + d, n_head)}, device_id_type=MESH
        )
    pl.semaphore_wait(barrier, partners)

    def near_copy(by, c, j):
        src = k_hbm if j == 0 else v_hbm
        i = 0 if by == 1 else 1
        return pltpu.make_async_remote_copy(
            src_ref=src.at[:, pl.ds(c * cw, cw)],
            dst_ref=kv.at[j, pl.ds(near_slot(by) * rows, rows), pl.ds(c * cw, cw)],
            send_sem=near_send.at[i, c, j],
            recv_sem=near_recv.at[i, c, j],
            device_id={"seq": me + by},
            device_id_type=MESH,
        )

    def far_copy(by, c, j):
        i = 0 if by == 2 else 1
        return pltpu.make_async_remote_copy(
            src_ref=stage.at[i, j, :, pl.ds(c * cw, cw)],
            dst_ref=kv.at[j, pl.ds(far_slot(by) * rows, rows), pl.ds(c * cw, cw)],
            send_sem=far_send.at[i, c, j],
            recv_sem=far_recv.at[i, c, j],
            device_id={"seq": me + by},
            device_id_type=MESH,
        )

    def text_copy(by, step, j):
        i = 0 if by == 1 else 1
        at = (MOST - 1) - by * (step - 1)
        return pltpu.make_async_remote_copy(
            src_ref=text.at[j, pl.ds(at * trows, trows)],
            dst_ref=text.at[j, pl.ds((at - by) * trows, trows)],
            send_sem=text_send.at[i, step - 1, j],
            recv_sem=text_recv.at[i, step - 1, j],
            device_id={"seq": me + by},
            device_id_type=MESH,
        )

    def text_start(step):
        for by in (1, -1):

            @pl.when(exists(by) & exists(-by * (step - 1)))
            def _():
                for j in range(2):
                    text_copy(by, step, j).start()

    def text_arrive(step):
        for by in (1, -1):

            @pl.when(exists(-by * step))
            def _():
                for j in range(2):
                    text_copy(by, step, j).wait_recv()

    for copy in own_copies[3:]:
        copy.wait()
    text_start(1)
    for c in range(chunks):
        for by in (1, -1):

            @pl.when(exists(by))
            def _():
                for j in range(2):
                    near_copy(by, c, j).start()

    def listed(tile):
        found = near_ref[0, 0] == tile
        for i in range(1, near_ref.shape[1]):
            found = found | (near_ref[0, i] == tile)
        return (found & (tile >= 0)).astype(jnp.int32)

    start = jnp.int32(0)
    clip_start = jnp.int32(0)
    clip_text = jnp.int32(0)
    for c in range(clip_ref.shape[0]):
        length = clip_ref[c]
        inside = ((start <= me) & (me < start + length)).astype(jnp.int32)
        clip_start = clip_start + inside * start
        clip_text = clip_text + inside * text_ref[c]
        start = start + length
    text_low = clip_start * trows
    text_high = text_low + clip_text

    def bias_of(flag):
        return (1.0 - flag.astype(jnp.float32)) * LOW

    bias_own = jnp.zeros((1, rows), jnp.float32)
    bias_near = [jnp.full((1, rows), bias_of(listed(me - by)), jnp.float32) for by in (1, -1)]
    bias_far = [
        jnp.full(
            (1, rows), bias_of(jnp.maximum(listed(me - by), listed(me - by - by // 2))), jnp.float32
        )
        for by in (2, -2)
    ]
    place = lax.broadcasted_iota(jnp.int32, (1, text_pad), 1)
    row = (me - (MOST - 1)) * trows + place
    owned = (row >= text_low) & (row < text_high) & (place < SPAN * trows)
    bias_text = jnp.where(owned, 0.0, LOW)
    bias_one = jnp.concatenate([bias_own] + bias_near, axis=1)
    bias_two = jnp.concatenate(bias_far, axis=1)
    own_share = [jnp.full((16, cw), listed(me + by).astype(jnp.float32)) for by in (2, -2)]

    scale = HD ** (-0.5) * 1.4426950408889634
    block = 128 if rows % 128 == 0 else rows
    blocks = rows // block

    def score(q_part, k_part, bias):
        s = lax.dot_general(
            q_part, k_part, (((1,), (1,)), ((), ())), preferred_element_type=jnp.float32
        )
        return s * scale + bias

    def weigh(p, v_part):
        return jnp.dot(p.astype(jnp.bfloat16), v_part, preferred_element_type=jnp.float32)

    def first(c):
        def one(i, carry):
            h = c * group + i // blocks
            at = pl.ds(pl.multiple_of(h * HD, HD), HD)
            qr = pl.ds(pl.multiple_of(lax.rem(i, blocks) * block, block), block)
            s = score(q[qr, at], kv[0, pl.ds(0, 3 * rows), at], bias_one)
            m = jnp.max(s, axis=1, keepdims=True)
            p = jnp.exp2(s - m)
            top[qr, at] = jnp.broadcast_to(m, (block, HD))
            total[qr, at] = jnp.broadcast_to(jnp.sum(p, axis=1, keepdims=True), (block, HD))
            acc[qr, at] = weigh(p, kv[1, pl.ds(0, 3 * rows), at])
            return carry

        lax.fori_loop(0, group * blocks, one, 0)

    def second(c):
        def one(i, carry):
            h = c * group + i // blocks
            at = pl.ds(pl.multiple_of(h * HD, HD), HD)
            qr = pl.ds(pl.multiple_of(lax.rem(i, blocks) * block, block), block)
            q_part = q[qr, at]
            far = pl.ds(3 * rows, 2 * rows)
            s1 = score(q_part, kv[0, far, at], bias_two)
            s2 = score(q_part, text[0, :, at], bias_text)
            before = top[qr, at]
            m = jnp.maximum(
                jnp.maximum(jnp.max(s1, axis=1, keepdims=True), jnp.max(s2, axis=1, keepdims=True)),
                before,
            )
            fade = jnp.exp2(before - m)
            p1 = jnp.exp2(s1 - m[:, :1])
            p2 = jnp.exp2(s2 - m[:, :1])
            l = (
                total[qr, at] * fade
                + jnp.sum(p1, axis=1, keepdims=True)
                + jnp.sum(p2, axis=1, keepdims=True)
            )
            a = acc[qr, at] * fade + weigh(p1, kv[1, far, at]) + weigh(p2, text[1, :, at])
            attended[qr, at] = (a / l).astype(jnp.bfloat16)
            return carry

        lax.fori_loop(0, group * blocks, one, 0)

    for copy in own_copies[:3]:
        copy.wait()

    step = 1
    for c in range(chunks):
        for by in (1, -1):

            @pl.when(exists(-by))
            def _():
                for j in range(2):
                    near_copy(by, c, j).wait_recv()

        cols = pl.ds(c * cw, cw)
        for i, by in enumerate((1, -1)):

            @pl.when(exists(2 * by))
            def _():
                def mix(r, carry):
                    mine = own_share[i].astype(jnp.bfloat16)
                    for j in range(2):
                        a = kv[j, pl.ds(pl.multiple_of(r * 16, 16), 16), cols]
                        b = kv[
                            j, pl.ds(pl.multiple_of(near_slot(by) * rows + r * 16, 16), 16), cols
                        ]
                        stage[i, j, pl.ds(pl.multiple_of(r * 16, 16), 16), cols] = (
                            a * mine + b * (1 - mine)
                        )
                    return carry

                lax.fori_loop(0, rows // 16, mix, 0)
                for j in range(2):
                    far_copy(2 * by, c, j).start()

        for _ in range(2 if c == 0 else 1):
            if step < MOST - 1:
                text_arrive(step)
                step += 1
                text_start(step)
        first(c)
    while step < MOST - 1:
        text_arrive(step)
        step += 1
        text_start(step)
    text_arrive(MOST - 1)

    for c in range(chunks):
        for by in (2, -2):

            @pl.when(exists(-by))
            def _():
                for j in range(2):
                    far_copy(by, c, j).wait_recv()

        second(c)

    w_copy.wait()
    wide = w.shape[1]
    parts = 4
    pw = wide // parts
    out_rows = rows // n_head

    def out_copy(d, p):
        peer = lax.rem(head + d, n_head)
        return pltpu.make_async_remote_copy(
            src_ref=partial.at[peer, :, pl.ds(p * pw, pw)],
            dst_ref=arrived.at[d - 1, :, pl.ds(p * pw, pw)],
            send_sem=out_send.at[d - 1, p],
            recv_sem=out_recv.at[d - 1, p],
            device_id={"head": peer},
            device_id_type=MESH,
        )

    for p in range(parts):
        for g in range(n_head):
            partial[g, :, pl.ds(p * pw, pw)] = jnp.dot(
                attended[pl.ds(g * out_rows, out_rows), :],
                w[:, pl.ds(p * pw, pw)],
                preferred_element_type=jnp.float32,
            ).astype(jnp.bfloat16)
        for d in range(1, n_head):
            out_copy(d, p).start()
    for p in range(parts):
        sums = partial[head, :, pl.ds(p * pw, pw)].astype(jnp.float32)
        for d in range(1, n_head):
            out_copy(d, p).wait_recv()
            sums = sums + arrived[d - 1, :, pl.ds(p * pw, pw)].astype(jnp.float32)
        out_ref[:, pl.ds(p * pw, pw)] = sums.astype(jnp.bfloat16)

    for by in (1, -1):

        @pl.when(exists(by))
        def _():
            for c in range(chunks):
                for j in range(2):
                    near_copy(by, c, j).wait_send()

        @pl.when(exists(2 * by))
        def _():
            for c in range(chunks):
                for j in range(2):
                    far_copy(2 * by, c, j).wait_send()

        for s in range(1, MOST):

            @pl.when(exists(by) & exists(-by * (s - 1)))
            def _():
                for j in range(2):
                    text_copy(by, s, j).wait_send()

    for p in range(parts):
        for d in range(1, n_head):
            out_copy(d, p).wait_send()


def body(n_seq, n_head, q, k, v, tk, tv, near, clip_lengths, text_lengths, w):
    rows, width = q.shape
    heads = width // HD
    group = GROUP if heads % GROUP == 0 else 1
    chunks = heads // group
    wide = w.shape[1]
    out_rows = rows // n_head
    text_pad = -(-SPAN * tk.shape[0] // 128) * 128
    smem = pl.BlockSpec(memory_space=pltpu.SMEM)
    hbm = pl.BlockSpec(memory_space=pl.ANY)
    dma = pltpu.SemaphoreType.DMA
    bf16, f32 = jnp.bfloat16, jnp.float32
    return pl.pallas_call(
        functools.partial(kernel, n_seq, n_head),
        out_shape=jax.ShapeDtypeStruct((out_rows, wide), bf16),
        in_specs=[smem] * 3 + [hbm] * 6,
        out_specs=pl.BlockSpec(memory_space=pltpu.VMEM),
        scratch_shapes=[
            pltpu.VMEM((rows, width), bf16),
            pltpu.VMEM((2, 5 * rows, width), bf16),
            pltpu.VMEM((2, text_pad, width), bf16),
            pltpu.VMEM((2, 2, rows, width), bf16),
            pltpu.VMEM(w.shape, bf16),
            pltpu.VMEM((rows, width), f32),
            pltpu.VMEM((rows, width), f32),
            pltpu.VMEM((rows, width), f32),
            pltpu.VMEM((rows, width), bf16),
            pltpu.VMEM((n_head, out_rows, wide), bf16),
            pltpu.VMEM((n_head - 1, out_rows, wide), bf16),
            dma((2, chunks, 2)),
            dma((2, chunks, 2)),
            dma((2, chunks, 2)),
            dma((2, chunks, 2)),
            dma((2, MOST - 1, 2)),
            dma((2, MOST - 1, 2)),
            dma((n_head - 1, 4)),
            dma((n_head - 1, 4)),
            dma((6,)),
        ],
        compiler_params=pltpu.CompilerParams(
            collective_id=0, has_side_effects=True, vmem_limit_bytes=58 << 20
        ),
    )(near, clip_lengths, text_lengths, q, k, v, tk, tv, w)


def solution(mesh):
    placed = (
        P("seq", "head"),
        P("seq", "head"),
        P("seq", "head"),
        P("seq", "head"),
        P("seq", "head"),
        P("seq", None),
        P(),
        P(),
        P("head", None),
    )
    return jax.shard_map(
        functools.partial(body, mesh.shape["seq"], mesh.shape["head"]),
        mesh=mesh,
        in_specs=placed,
        out_specs=P(("seq", "head"), None),
        check_vma=False,
    )
```

```python
import functools

import jax
import jax.numpy as jnp
from jax import lax
from jax.experimental import pallas as pl
from jax.experimental.pallas import tpu as pltpu
from jax.sharding import PartitionSpec as P

HD = 128
MOST = 7
PLANE = 4
PLANES_AROUND = 2
COLUMN = 2 * PLANES_AROUND + 1
GROUP = 2
LOW = -1e30
MESH = pl.DeviceIdType.MESH


def kernel(
    n_seq,
    n_head,
    near_ref,
    clip_ref,
    text_ref,
    q_hbm,
    k_hbm,
    v_hbm,
    tk_hbm,
    tv_hbm,
    w_hbm,
    list_hbm,
    out_ref,
    q,
    kv,
    text,
    stage,
    w,
    acc,
    top,
    total,
    attended,
    partial,
    arrived,
    passed,
    peer_list,
    near_send,
    near_recv,
    edge_send,
    edge_recv,
    far_send,
    far_recv,
    text_send,
    text_recv,
    pass_send,
    pass_recv,
    list_sem,
    out_send,
    out_recv,
    local_sem,
):
    me = lax.axis_index("seq")
    head = lax.axis_index("head")
    rows, width = q.shape
    heads = width // HD
    group = GROUP if heads % GROUP == 0 else 1
    chunks = heads // group
    cw = group * HD
    trows = tk_hbm.shape[0]
    text_pad = text.shape[1]
    j4 = lax.rem(me, PLANE)
    base = me - j4
    low_half = j4 < PLANE // 2

    def exists(by):
        return (me + by >= 0) & (me + by < n_seq)

    def side(i):
        return low_half if i == 0 else jnp.logical_not(low_half)

    def at_place(by, place):
        return j4 == (place if by == 1 else PLANE - 1 - place)

    def near_slot(by):
        return 1 if by == 1 else 2

    def far_slot(by):
        return 3 if by == 1 else 4

    mid = PLANES_AROUND * trows
    own_copies = [
        pltpu.make_async_copy(q_hbm, q, local_sem.at[0]),
        pltpu.make_async_copy(k_hbm, kv.at[0, pl.ds(0, rows)], local_sem.at[1]),
        pltpu.make_async_copy(v_hbm, kv.at[1, pl.ds(0, rows)], local_sem.at[2]),
        pltpu.make_async_copy(tk_hbm, text.at[0, pl.ds(mid, trows)], local_sem.at[3]),
        pltpu.make_async_copy(tv_hbm, text.at[1, pl.ds(mid, trows)], local_sem.at[4]),
    ]
    w_copy = pltpu.make_async_copy(w_hbm, w, local_sem.at[5])
    text[...] = jnp.zeros_like(text)
    for copy in own_copies:
        copy.start()

    def blank(slot):
        kv[:, pl.ds(slot * rows, rows), :] = jnp.zeros((2, rows, width), kv.dtype)

    for by in (1, -1):

        @pl.when(jnp.logical_not(exists(-by)))
        def _():
            blank(near_slot(by))

        @pl.when(side(0 if by == 1 else 1) & jnp.logical_not(exists(-PLANE * by)))
        def _():
            blank(far_slot(by))

    peer_list[...] = jnp.full(peer_list.shape, -1, jnp.int32)

    barrier = pltpu.get_barrier_semaphore()
    partners = n_head - 1
    for step in (1, 2, 3, 4):
        for by in (step, -step):
            partners = partners + exists(by).astype(jnp.int32)

            @pl.when(exists(by))
            def _():
                pl.semaphore_signal(barrier, inc=1, device_id={"seq": me + by}, device_id_type=MESH)

    for d in range(1, n_head):
        pl.semaphore_signal(
            barrier, inc=1, device_id={"head": lax.rem(head + d, n_head)}, device_id_type=MESH
        )
    pl.semaphore_wait(barrier, partners)

    def push(src, dst, sem, at, to):
        return pltpu.make_async_remote_copy(
            src_ref=src,
            dst_ref=dst,
            send_sem=sem[0].at[at],
            recv_sem=sem[1].at[at],
            device_id={"seq": to},
            device_id_type=MESH,
        )

    near_sem = (near_send, near_recv)
    edge_sem = (edge_send, edge_recv)
    far_sem = (far_send, far_recv)
    text_sem = (text_send, text_recv)
    pass_sem = (pass_send, pass_recv)

    def slot_at(n, c, j):
        return kv.at[j, pl.ds(n * rows, rows), pl.ds(c * cw, cw)]

    def near_copy(by, c, j):
        src = (k_hbm if j == 0 else v_hbm).at[:, pl.ds(c * cw, cw)]
        i = 0 if by == 1 else 1
        return push(src, slot_at(near_slot(by), c, j), near_sem, (i, c, j), me + by)

    def edge_copy(by, c, j):
        i = 0 if by == 1 else 1
        src = slot_at(near_slot(-by), c, j)
        return push(src, slot_at(near_slot(by), c, j), edge_sem, (i, c, j), me + 2 * by)

    def far_copy(by, c, j):
        src = stage.at[0, j, :, pl.ds(c * cw, cw)]
        return push(src, slot_at(far_slot(by), c, j), far_sem, (0, c, j), me + 2 * by)

    def over_copy(by, c, j):
        src = stage.at[1, j, :, pl.ds(c * cw, cw)]
        return push(src, slot_at(far_slot(by), c, j), far_sem, (1, c, j), me + PLANE * by)

    def list_copy(by):
        return pltpu.make_async_remote_copy(
            src_ref=list_hbm,
            dst_ref=peer_list,
            send_sem=list_sem.at[0],
            recv_sem=list_sem.at[1],
            device_id={"seq": me - PLANE * by},
            device_id_type=MESH,
        )

    def column_copy(by, step, j):
        i = 0 if by == 1 else 1
        at = PLANES_AROUND - by * (step - 1)
        return push(
            text.at[j, pl.ds(at * trows, trows)],
            text.at[j, pl.ds((at - by) * trows, trows)],
            text_sem,
            (i, step - 1, j),
            me + PLANE * by,
        )

    def pass_copy(m, j):
        return push(
            passed.at[j, pl.ds((m - 1) * 2 * trows, 2 * trows)],
            text.at[j, pl.ds((COLUMN + 2 * (m - 1)) * trows, 2 * trows)],
            pass_sem,
            (m - 1, j),
            base + lax.rem(j4 + m, PLANE),
        )

    def column_start(step):
        for by in (1, -1):

            @pl.when(exists(PLANE * by) & exists(-PLANE * by * (step - 1)))
            def _():
                for j in range(2):
                    column_copy(by, step, j).start()

    def column_arrive(step):
        for by in (1, -1):

            @pl.when(exists(-PLANE * by * step))
            def _():
                for j in range(2):
                    column_copy(by, step, j).wait_recv()

    for copy in own_copies[3:]:
        copy.wait()
    for i, by in enumerate((1, -1)):

        @pl.when(side(i) & exists(-PLANE * by))
        def _():
            list_copy(by).start()

    column_start(1)
    for c in range(chunks):
        for by in (1, -1):

            @pl.when(jnp.logical_not(at_place(by, PLANE - 1)))
            def _():
                for j in range(2):
                    near_copy(by, c, j).start()

    w_copy.start()

    def listed(tile):
        found = near_ref[0, 0] == tile
        for i in range(1, near_ref.shape[1]):
            found = found | (near_ref[0, i] == tile)
        return (found & (tile >= 0)).astype(jnp.int32)

    def clip_of(tile):
        start = jnp.int32(0)
        first_tile = jnp.int32(0)
        count = jnp.int32(0)
        for c in range(clip_ref.shape[0]):
            length = clip_ref[c]
            inside = ((start <= tile) & (tile < start + length)).astype(jnp.int32)
            first_tile = first_tile + inside * start
            count = count + inside * text_ref[c]
            start = start + length
        return first_tile, count

    def in_column(first_tile, column):
        return first_tile + lax.rem(column + PLANE * n_seq - first_tile, PLANE)

    clip_start, clip_text = clip_of(me)
    text_low = clip_start * trows
    text_high = text_low + clip_text

    def bias_of(flag):
        return (1.0 - flag.astype(jnp.float32)) * LOW

    bias_own = jnp.zeros((1, rows), jnp.float32)
    bias_near = [jnp.full((1, rows), bias_of(listed(me - by)), jnp.float32) for by in (1, -1)]
    bias_far = [
        jnp.full(
            (1, rows), bias_of(jnp.maximum(listed(me - by), listed(me - by - by // 2))), jnp.float32
        )
        for by in (2, -2)
    ]
    place = lax.broadcasted_iota(jnp.int32, (1, text_pad), 1)
    shift = jnp.full((1, text_pad), -1, jnp.int32)
    tiles = [me + PLANE * (d - PLANES_AROUND) for d in range(COLUMN)]
    for m in range(1, PLANE):
        origin = in_column(clip_start, lax.rem(j4 + PLANE - m, PLANE))
        tiles += [origin, origin + PLANE]
    for n, tile in enumerate(tiles):
        here = (place >= n * trows) & (place < (n + 1) * trows)
        shift = jnp.where(here, (tile - n) * trows + place, shift)
    bias_text = jnp.where((shift >= text_low) & (shift < text_high), 0.0, LOW)
    bias_one = jnp.concatenate([bias_own] + bias_near, axis=1)
    bias_two = jnp.concatenate(bias_far, axis=1)
    own_share = jnp.full(
        (16, cw), jnp.maximum(listed(me + 2), listed(me - 2)).astype(jnp.float32)
    ).astype(jnp.bfloat16)

    scale = HD ** (-0.5) * 1.4426950408889634
    block = 128 if rows % 128 == 0 else rows
    blocks = rows // block

    def score(q_part, k_part, bias):
        s = lax.dot_general(
            q_part, k_part, (((1,), (1,)), ((), ())), preferred_element_type=jnp.float32
        )
        return s * scale + bias

    def weigh(p, v_part):
        return jnp.dot(p.astype(jnp.bfloat16), v_part, preferred_element_type=jnp.float32)

    def first(c):
        def one(i, carry):
            h = c * group + i // blocks
            at = pl.ds(pl.multiple_of(h * HD, HD), HD)
            qr = pl.ds(pl.multiple_of(lax.rem(i, blocks) * block, block), block)
            s = score(q[qr, at], kv[0, pl.ds(0, 3 * rows), at], bias_one)
            m = jnp.max(s, axis=1, keepdims=True)
            p = jnp.exp2(s - m)
            top[qr, at] = jnp.broadcast_to(m, (block, HD))
            total[qr, at] = jnp.broadcast_to(jnp.sum(p, axis=1, keepdims=True), (block, HD))
            acc[qr, at] = weigh(p, kv[1, pl.ds(0, 3 * rows), at])
            return carry

        lax.fori_loop(0, group * blocks, one, 0)

    def second(c):
        def one(i, carry):
            h = c * group + i // blocks
            at = pl.ds(pl.multiple_of(h * HD, HD), HD)
            qr = pl.ds(pl.multiple_of(lax.rem(i, blocks) * block, block), block)
            q_part = q[qr, at]
            far = pl.ds(3 * rows, 2 * rows)
            s1 = score(q_part, kv[0, far, at], bias_two)
            s2 = score(q_part, text[0, :, at], bias_text)
            before = top[qr, at]
            m = jnp.maximum(
                jnp.maximum(jnp.max(s1, axis=1, keepdims=True), jnp.max(s2, axis=1, keepdims=True)),
                before,
            )
            fade = jnp.exp2(before - m)
            p1 = jnp.exp2(s1 - m[:, :1])
            p2 = jnp.exp2(s2 - m[:, :1])
            l = (
                total[qr, at] * fade
                + jnp.sum(p1, axis=1, keepdims=True)
                + jnp.sum(p2, axis=1, keepdims=True)
            )
            a = acc[qr, at] * fade + weigh(p1, kv[1, far, at]) + weigh(p2, text[1, :, at])
            attended[qr, at] = (a / l).astype(jnp.bfloat16)
            return carry

        lax.fori_loop(0, group * blocks, one, 0)

    def pass_text():
        for m in range(1, PLANE):
            first_tile, _ = clip_of(base + lax.rem(j4 + m, PLANE))
            plane = lax.div(in_column(first_tile, j4) + PLANE * n_seq - me, PLANE) - n_seq
            for extra in range(2):
                for j in range(2):
                    picked = jnp.zeros((trows, width), jnp.bfloat16)
                    for d in range(COLUMN):
                        share = (plane + extra == d - PLANES_AROUND).astype(jnp.float32)
                        share = jnp.full((trows, width), share).astype(jnp.bfloat16)
                        picked = picked + share * text[j, pl.ds(d * trows, trows), :]
                    passed[j, pl.ds((2 * (m - 1) + extra) * trows, trows), :] = picked
            for j in range(2):
                pass_copy(m, j).start()

    def mix(share, n, slot_one, slot_two, c):
        cols = pl.ds(c * cw, cw)

        def one(r, carry):
            for j in range(2):
                a = kv[j, pl.ds(pl.multiple_of(slot_one * rows + r * 16, 16), 16), cols]
                b = kv[j, pl.ds(pl.multiple_of(slot_two * rows + r * 16, 16), 16), cols]
                stage[n, j, pl.ds(pl.multiple_of(r * 16, 16), 16), cols] = a * share + b * (
                    1 - share
                )
            return carry

        lax.fori_loop(0, rows // 16, one, 0)

    def near_stage(c):
        for by in (1, -1):

            @pl.when(jnp.logical_not(at_place(by, 0)))
            def _():
                for j in range(2):
                    near_copy(by, c, j).wait_recv()

        for by in (1, -1):

            @pl.when(at_place(by, PLANE - 2) & exists(2 * by))
            def _():
                for j in range(2):
                    edge_copy(by, c, j).start()

    def far_stage(c):
        for i, by in enumerate((1, -1)):

            @pl.when(at_place(by, 0) & exists(-by))
            def _():
                for j in range(2):
                    edge_copy(by, c, j).wait_recv()

        for i, by in enumerate((1, -1)):

            @pl.when(side(i))
            def _():
                mix(own_share, 0, 0, near_slot(by), c)
                for j in range(2):
                    far_copy(by, c, j).start()

    def over_stage(c):
        for i, by in enumerate((1, -1)):

            @pl.when(side(i))
            def _():
                for j in range(2):
                    far_copy(-by, c, j).wait_recv()

            @pl.when(side(i) & exists(PLANE * by))
            def _():
                wanted = (peer_list[...] == me + 2 * by).astype(jnp.float32)
                wanted = jnp.max(jnp.max(wanted, axis=1, keepdims=True), axis=0, keepdims=True)
                share = jnp.broadcast_to(wanted, (16, cw)).astype(jnp.bfloat16)
                mix(share, 1, far_slot(-by), near_slot(-by), c)
                for j in range(2):
                    over_copy(by, c, j).start()

    def last_stage(c):
        for i, by in enumerate((1, -1)):

            @pl.when(side(i) & exists(-PLANE * by))
            def _():
                for j in range(2):
                    over_copy(by, c, j).wait_recv()

    column_arrive(1)
    column_start(2)
    for copy in own_copies[:3]:
        copy.wait()
    for i, by in enumerate((1, -1)):

        @pl.when(side(i) & exists(PLANE * by))
        def _():
            list_copy(by).wait_recv()

    for turn in range(chunks + 3):
        if turn < chunks:
            near_stage(turn)
        if 0 <= turn - 1 < chunks:
            far_stage(turn - 1)
        if turn == 1:
            column_arrive(2)
            pass_text()
        if 0 <= turn - 2 < chunks:
            over_stage(turn - 2)
        if 0 <= turn - 1 < chunks:
            first(turn - 1)
        if turn == 3:
            for m in range(1, PLANE):
                for j in range(2):
                    pass_copy(m, j).wait_recv()
        if 0 <= turn - 3:
            last_stage(turn - 3)
            second(turn - 3)

    w_copy.wait()
    wide = w.shape[1]
    parts = 4
    pw = wide // parts
    out_rows = rows // n_head

    def out_copy(d, p):
        peer = lax.rem(head + d, n_head)
        return pltpu.make_async_remote_copy(
            src_ref=partial.at[peer, :, pl.ds(p * pw, pw)],
            dst_ref=arrived.at[d - 1, :, pl.ds(p * pw, pw)],
            send_sem=out_send.at[d - 1, p],
            recv_sem=out_recv.at[d - 1, p],
            device_id={"head": peer},
            device_id_type=MESH,
        )

    for p in range(parts):
        for g in range(n_head):
            partial[g, :, pl.ds(p * pw, pw)] = jnp.dot(
                attended[pl.ds(g * out_rows, out_rows), :],
                w[:, pl.ds(p * pw, pw)],
                preferred_element_type=jnp.float32,
            ).astype(jnp.bfloat16)
        for d in range(1, n_head):
            out_copy(d, p).start()
    for p in range(parts):
        sums = partial[head, :, pl.ds(p * pw, pw)].astype(jnp.float32)
        for d in range(1, n_head):
            out_copy(d, p).wait_recv()
            sums = sums + arrived[d - 1, :, pl.ds(p * pw, pw)].astype(jnp.float32)
        out_ref[:, pl.ds(p * pw, pw)] = sums.astype(jnp.bfloat16)

    for i, by in enumerate((1, -1)):

        @pl.when(side(i) & exists(-PLANE * by))
        def _():
            list_copy(by).wait_send()

        @pl.when(jnp.logical_not(at_place(by, PLANE - 1)))
        def _():
            for c in range(chunks):
                for j in range(2):
                    near_copy(by, c, j).wait_send()

        @pl.when(at_place(by, PLANE - 2) & exists(2 * by))
        def _():
            for c in range(chunks):
                for j in range(2):
                    edge_copy(by, c, j).wait_send()

        @pl.when(side(i))
        def _():
            for c in range(chunks):
                for j in range(2):
                    far_copy(by, c, j).wait_send()

        @pl.when(side(i) & exists(PLANE * by))
        def _():
            for c in range(chunks):
                for j in range(2):
                    over_copy(by, c, j).wait_send()

        for step in range(1, PLANES_AROUND + 1):

            @pl.when(exists(PLANE * by) & exists(-PLANE * by * (step - 1)))
            def _():
                for j in range(2):
                    column_copy(by, step, j).wait_send()

    for m in range(1, PLANE):
        for j in range(2):
            pass_copy(m, j).wait_send()

    for p in range(parts):
        for d in range(1, n_head):
            out_copy(d, p).wait_send()


def body(n_seq, n_head, q, k, v, tk, tv, near, clip_lengths, text_lengths, w):
    rows, width = q.shape
    heads = width // HD
    group = GROUP if heads % GROUP == 0 else 1
    chunks = heads // group
    wide = w.shape[1]
    out_rows = rows // n_head
    trows = tk.shape[0]
    text_pad = -(-(COLUMN + 2 * (PLANE - 1)) * trows // 128) * 128
    padded = jnp.pad(near, ((0, 7), (0, 128 - near.shape[1])), constant_values=-1)
    smem = pl.BlockSpec(memory_space=pltpu.SMEM)
    hbm = pl.BlockSpec(memory_space=pl.ANY)
    dma = pltpu.SemaphoreType.DMA
    bf16, f32 = jnp.bfloat16, jnp.float32
    return pl.pallas_call(
        functools.partial(kernel, n_seq, n_head),
        out_shape=jax.ShapeDtypeStruct((out_rows, wide), bf16),
        in_specs=[smem] * 3 + [hbm] * 7,
        out_specs=pl.BlockSpec(memory_space=pltpu.VMEM),
        scratch_shapes=[
            pltpu.VMEM((rows, width), bf16),
            pltpu.VMEM((2, 5 * rows, width), bf16),
            pltpu.VMEM((2, text_pad, width), bf16),
            pltpu.VMEM((2, 2, rows, width), bf16),
            pltpu.VMEM(w.shape, bf16),
            pltpu.VMEM((rows, width), f32),
            pltpu.VMEM((rows, width), f32),
            pltpu.VMEM((rows, width), f32),
            pltpu.VMEM((rows, width), bf16),
            pltpu.VMEM((n_head, out_rows, wide), bf16),
            pltpu.VMEM((n_head - 1, out_rows, wide), bf16),
            pltpu.VMEM((2, 2 * (PLANE - 1) * trows, width), bf16),
            pltpu.VMEM((8, 128), jnp.int32),
            dma((2, chunks, 2)),
            dma((2, chunks, 2)),
            dma((2, chunks, 2)),
            dma((2, chunks, 2)),
            dma((2, chunks, 2)),
            dma((2, chunks, 2)),
            dma((2, PLANES_AROUND, 2)),
            dma((2, PLANES_AROUND, 2)),
            dma((PLANE - 1, 2)),
            dma((PLANE - 1, 2)),
            dma((2,)),
            dma((n_head - 1, 4)),
            dma((n_head - 1, 4)),
            dma((6,)),
        ],
        compiler_params=pltpu.CompilerParams(
            collective_id=0, has_side_effects=True, vmem_limit_bytes=58 << 20
        ),
    )(near, clip_lengths, text_lengths, q, k, v, tk, tv, w, padded)


def solution(mesh):
    placed = (
        P("seq", "head"),
        P("seq", "head"),
        P("seq", "head"),
        P("seq", "head"),
        P("seq", "head"),
        P("seq", None),
        P(),
        P(),
        P("head", None),
    )
    return jax.shard_map(
        functools.partial(body, mesh.shape["seq"], mesh.shape["head"]),
        mesh=mesh,
        in_specs=placed,
        out_specs=P(("seq", "head"), None),
        check_vma=False,
    )
```

```python
import functools

import jax
import jax.numpy as jnp
from jax import lax
from jax.experimental import pallas as pl
from jax.experimental.pallas import tpu as pltpu
from jax.sharding import PartitionSpec as P

HD = 128
MOST = 7
PLANE = 4
PLANES_AROUND = 2
COLUMN = 2 * PLANES_AROUND + 1
GROUP = 2
AHEAD = 2
LOW = -1e30
MESH = pl.DeviceIdType.MESH


def kernel(
    n_seq,
    n_head,
    near_ref,
    clip_ref,
    text_ref,
    q_hbm,
    k_hbm,
    v_hbm,
    tk_hbm,
    tv_hbm,
    w_hbm,
    list_hbm,
    out_ref,
    q,
    kv,
    text,
    stage,
    w,
    acc,
    top,
    total,
    attended,
    partial,
    arrived,
    passed,
    peer_list,
    near_send,
    near_recv,
    edge_send,
    edge_recv,
    far_send,
    far_recv,
    text_send,
    text_recv,
    pass_send,
    pass_recv,
    list_sem,
    out_send,
    out_recv,
    local_sem,
):
    me = lax.axis_index("seq")
    head = lax.axis_index("head")
    rows, width = q.shape
    heads = width // HD
    group = GROUP if heads % GROUP == 0 else 1
    chunks = heads // group
    cw = group * HD
    trows = tk_hbm.shape[0]
    text_pad = text.shape[1]
    j4 = lax.rem(me, PLANE)
    base = me - j4
    low_half = j4 < PLANE // 2

    def exists(by):
        return (me + by >= 0) & (me + by < n_seq)

    def side(i):
        return low_half if i == 0 else jnp.logical_not(low_half)

    def at_place(by, place):
        return j4 == (place if by == 1 else PLANE - 1 - place)

    def near_slot(by):
        return 1 if by == 1 else 2

    def far_slot(by):
        return 3 if by == 1 else 4

    mid = PLANES_AROUND * trows
    own_copies = [
        pltpu.make_async_copy(q_hbm, q, local_sem.at[0]),
        pltpu.make_async_copy(k_hbm, kv.at[0, pl.ds(0, rows)], local_sem.at[1]),
        pltpu.make_async_copy(v_hbm, kv.at[1, pl.ds(0, rows)], local_sem.at[2]),
        pltpu.make_async_copy(tk_hbm, text.at[0, pl.ds(mid, trows)], local_sem.at[3]),
        pltpu.make_async_copy(tv_hbm, text.at[1, pl.ds(mid, trows)], local_sem.at[4]),
    ]
    w_copy = pltpu.make_async_copy(w_hbm, w, local_sem.at[5])
    text[...] = jnp.zeros_like(text)
    for copy in own_copies:
        copy.start()

    def blank(slot):
        kv[:, pl.ds(slot * rows, rows), :] = jnp.zeros((2, rows, width), kv.dtype)

    for by in (1, -1):

        @pl.when(jnp.logical_not(exists(-by)))
        def _():
            blank(near_slot(by))

        @pl.when(side(0 if by == 1 else 1) & jnp.logical_not(exists(-PLANE * by)))
        def _():
            blank(far_slot(by))

    peer_list[...] = jnp.full(peer_list.shape, -1, jnp.int32)

    barrier = pltpu.get_barrier_semaphore()
    partners = n_head - 1
    for step in (1, 2, 3, 4):
        for by in (step, -step):
            partners = partners + exists(by).astype(jnp.int32)

            @pl.when(exists(by))
            def _():
                pl.semaphore_signal(barrier, inc=1, device_id={"seq": me + by}, device_id_type=MESH)

    for d in range(1, n_head):
        pl.semaphore_signal(
            barrier, inc=1, device_id={"head": lax.rem(head + d, n_head)}, device_id_type=MESH
        )
    pl.semaphore_wait(barrier, partners)

    def push(src, dst, sem, at, to):
        return pltpu.make_async_remote_copy(
            src_ref=src,
            dst_ref=dst,
            send_sem=sem[0].at[at],
            recv_sem=sem[1].at[at],
            device_id={"seq": to},
            device_id_type=MESH,
        )

    near_sem = (near_send, near_recv)
    edge_sem = (edge_send, edge_recv)
    far_sem = (far_send, far_recv)
    text_sem = (text_send, text_recv)
    pass_sem = (pass_send, pass_recv)

    def slot_at(n, c, j):
        return kv.at[j, pl.ds(n * rows, rows), pl.ds(c * cw, cw)]

    def near_copy(by, c, j):
        src = (k_hbm if j == 0 else v_hbm).at[:, pl.ds(c * cw, cw)]
        i = 0 if by == 1 else 1
        return push(src, slot_at(near_slot(by), c, j), near_sem, (i, c, j), me + by)

    def edge_copy(by, c, j):
        i = 0 if by == 1 else 1
        src = slot_at(near_slot(-by), c, j)
        return push(src, slot_at(near_slot(by), c, j), edge_sem, (i, c, j), me + 2 * by)

    def far_copy(by, c, j):
        src = stage.at[0, j, :, pl.ds(c * cw, cw)]
        return push(src, slot_at(far_slot(by), c, j), far_sem, (0, c, j), me + 2 * by)

    def over_copy(by, c, j):
        src = stage.at[1, j, :, pl.ds(c * cw, cw)]
        return push(src, slot_at(far_slot(by), c, j), far_sem, (1, c, j), me + PLANE * by)

    def list_copy(by):
        return pltpu.make_async_remote_copy(
            src_ref=list_hbm,
            dst_ref=peer_list,
            send_sem=list_sem.at[0],
            recv_sem=list_sem.at[1],
            device_id={"seq": me - PLANE * by},
            device_id_type=MESH,
        )

    def column_copy(by, step, j):
        i = 0 if by == 1 else 1
        at = PLANES_AROUND - by * (step - 1)
        return push(
            text.at[j, pl.ds(at * trows, trows)],
            text.at[j, pl.ds((at - by) * trows, trows)],
            text_sem,
            (i, step - 1, j),
            me + PLANE * by,
        )

    def pass_copy(m, j):
        return push(
            passed.at[j, pl.ds((m - 1) * 2 * trows, 2 * trows)],
            text.at[j, pl.ds((COLUMN + 2 * (m - 1)) * trows, 2 * trows)],
            pass_sem,
            (m - 1, j),
            base + lax.rem(j4 + m, PLANE),
        )

    def column_start(step):
        for by in (1, -1):

            @pl.when(exists(PLANE * by) & exists(-PLANE * by * (step - 1)))
            def _():
                for j in range(2):
                    column_copy(by, step, j).start()

    def column_arrive(step):
        for by in (1, -1):

            @pl.when(exists(-PLANE * by * step))
            def _():
                for j in range(2):
                    column_copy(by, step, j).wait_recv()

    for copy in own_copies[3:]:
        copy.wait()
    for i, by in enumerate((1, -1)):

        @pl.when(side(i) & exists(-PLANE * by))
        def _():
            list_copy(by).start()

    column_start(1)
    def near_start(c):
        for by in (1, -1):

            @pl.when(jnp.logical_not(at_place(by, PLANE - 1)))
            def _():
                for j in range(2):
                    near_copy(by, c, j).start()

    for c in range(min(AHEAD, chunks)):
        near_start(c)
    w_copy.start()

    def listed(tile):
        found = near_ref[0, 0] == tile
        for i in range(1, near_ref.shape[1]):
            found = found | (near_ref[0, i] == tile)
        return (found & (tile >= 0)).astype(jnp.int32)

    def clip_of(tile):
        start = jnp.int32(0)
        first_tile = jnp.int32(0)
        count = jnp.int32(0)
        for c in range(clip_ref.shape[0]):
            length = clip_ref[c]
            inside = ((start <= tile) & (tile < start + length)).astype(jnp.int32)
            first_tile = first_tile + inside * start
            count = count + inside * text_ref[c]
            start = start + length
        return first_tile, count

    def in_column(first_tile, column):
        return first_tile + lax.rem(column + PLANE * n_seq - first_tile, PLANE)

    clip_start, clip_text = clip_of(me)
    text_low = clip_start * trows
    text_high = text_low + clip_text

    def bias_of(flag):
        return (1.0 - flag.astype(jnp.float32)) * LOW

    bias_own = jnp.zeros((1, rows), jnp.float32)
    bias_near = [jnp.full((1, rows), bias_of(listed(me - by)), jnp.float32) for by in (1, -1)]
    bias_far = [
        jnp.full(
            (1, rows), bias_of(jnp.maximum(listed(me - by), listed(me - by - by // 2))), jnp.float32
        )
        for by in (2, -2)
    ]
    place = lax.broadcasted_iota(jnp.int32, (1, text_pad), 1)
    shift = jnp.full((1, text_pad), -1, jnp.int32)
    tiles = [me + PLANE * (d - PLANES_AROUND) for d in range(COLUMN)]
    for m in range(1, PLANE):
        origin = in_column(clip_start, lax.rem(j4 + PLANE - m, PLANE))
        tiles += [origin, origin + PLANE]
    for n, tile in enumerate(tiles):
        here = (place >= n * trows) & (place < (n + 1) * trows)
        shift = jnp.where(here, (tile - n) * trows + place, shift)
    bias_text = jnp.where((shift >= text_low) & (shift < text_high), 0.0, LOW)
    bias_one = jnp.concatenate([bias_own] + bias_near, axis=1)
    bias_two = jnp.concatenate(bias_far, axis=1)
    own_share = jnp.full(
        (16, cw), jnp.maximum(listed(me + 2), listed(me - 2)).astype(jnp.float32)
    ).astype(jnp.bfloat16)

    scale = HD ** (-0.5) * 1.4426950408889634
    block = 128 if rows % 128 == 0 else rows
    blocks = rows // block

    def score(q_part, k_part, bias):
        s = lax.dot_general(
            q_part, k_part, (((1,), (1,)), ((), ())), preferred_element_type=jnp.float32
        )
        return s * scale + bias

    def weigh(p, v_part):
        return jnp.dot(p.astype(jnp.bfloat16), v_part, preferred_element_type=jnp.float32)

    def first(c):
        def one(i, carry):
            h = c * group + i // blocks
            at = pl.ds(pl.multiple_of(h * HD, HD), HD)
            qr = pl.ds(pl.multiple_of(lax.rem(i, blocks) * block, block), block)
            s = score(q[qr, at], kv[0, pl.ds(0, 3 * rows), at], bias_one)
            m = jnp.max(s, axis=1, keepdims=True)
            p = jnp.exp2(s - m)
            top[qr, at] = jnp.broadcast_to(m, (block, HD))
            total[qr, at] = jnp.broadcast_to(jnp.sum(p, axis=1, keepdims=True), (block, HD))
            acc[qr, at] = weigh(p, kv[1, pl.ds(0, 3 * rows), at])
            return carry

        lax.fori_loop(0, group * blocks, one, 0)

    def second(c):
        def one(i, carry):
            h = c * group + i // blocks
            at = pl.ds(pl.multiple_of(h * HD, HD), HD)
            qr = pl.ds(pl.multiple_of(lax.rem(i, blocks) * block, block), block)
            q_part = q[qr, at]
            far = pl.ds(3 * rows, 2 * rows)
            s1 = score(q_part, kv[0, far, at], bias_two)
            s2 = score(q_part, text[0, :, at], bias_text)
            before = top[qr, at]
            m = jnp.maximum(
                jnp.maximum(jnp.max(s1, axis=1, keepdims=True), jnp.max(s2, axis=1, keepdims=True)),
                before,
            )
            fade = jnp.exp2(before - m)
            p1 = jnp.exp2(s1 - m[:, :1])
            p2 = jnp.exp2(s2 - m[:, :1])
            l = (
                total[qr, at] * fade
                + jnp.sum(p1, axis=1, keepdims=True)
                + jnp.sum(p2, axis=1, keepdims=True)
            )
            a = acc[qr, at] * fade + weigh(p1, kv[1, far, at]) + weigh(p2, text[1, :, at])
            attended[qr, at] = (a / l).astype(jnp.bfloat16)
            return carry

        lax.fori_loop(0, group * blocks, one, 0)

    def pass_text():
        for m in range(1, PLANE):
            first_tile, _ = clip_of(base + lax.rem(j4 + m, PLANE))
            plane = lax.div(in_column(first_tile, j4) + PLANE * n_seq - me, PLANE) - n_seq
            for extra in range(2):
                for j in range(2):
                    picked = jnp.zeros((trows, width), jnp.bfloat16)
                    for d in range(COLUMN):
                        share = (plane + extra == d - PLANES_AROUND).astype(jnp.float32)
                        share = jnp.full((trows, width), share).astype(jnp.bfloat16)
                        picked = picked + share * text[j, pl.ds(d * trows, trows), :]
                    passed[j, pl.ds((2 * (m - 1) + extra) * trows, trows), :] = picked
            for j in range(2):
                pass_copy(m, j).start()

    def mix(share, n, slot_one, slot_two, c):
        cols = pl.ds(c * cw, cw)

        def one(r, carry):
            for j in range(2):
                a = kv[j, pl.ds(pl.multiple_of(slot_one * rows + r * 16, 16), 16), cols]
                b = kv[j, pl.ds(pl.multiple_of(slot_two * rows + r * 16, 16), 16), cols]
                stage[n, j, pl.ds(pl.multiple_of(r * 16, 16), 16), cols] = a * share + b * (
                    1 - share
                )
            return carry

        lax.fori_loop(0, rows // 16, one, 0)

    def near_stage(c):
        for by in (1, -1):

            @pl.when(jnp.logical_not(at_place(by, 0)))
            def _():
                for j in range(2):
                    near_copy(by, c, j).wait_recv()

        for by in (1, -1):

            @pl.when(at_place(by, PLANE - 2) & exists(2 * by))
            def _():
                for j in range(2):
                    edge_copy(by, c, j).start()

    def far_stage(c):
        for i, by in enumerate((1, -1)):

            @pl.when(at_place(by, 0) & exists(-by))
            def _():
                for j in range(2):
                    edge_copy(by, c, j).wait_recv()

        for i, by in enumerate((1, -1)):

            @pl.when(side(i))
            def _():
                mix(own_share, 0, 0, near_slot(by), c)
                for j in range(2):
                    far_copy(by, c, j).start()

    def over_stage(c):
        for i, by in enumerate((1, -1)):

            @pl.when(side(i))
            def _():
                for j in range(2):
                    far_copy(-by, c, j).wait_recv()

            @pl.when(side(i) & exists(PLANE * by))
            def _():
                wanted = (peer_list[...] == me + 2 * by).astype(jnp.float32)
                wanted = jnp.max(jnp.max(wanted, axis=1, keepdims=True), axis=0, keepdims=True)
                share = jnp.broadcast_to(wanted, (16, cw)).astype(jnp.bfloat16)
                mix(share, 1, far_slot(-by), near_slot(-by), c)
                for j in range(2):
                    over_copy(by, c, j).start()

    def last_stage(c):
        for i, by in enumerate((1, -1)):

            @pl.when(side(i) & exists(-PLANE * by))
            def _():
                for j in range(2):
                    over_copy(by, c, j).wait_recv()

    column_arrive(1)
    column_start(2)
    for copy in own_copies[:3]:
        copy.wait()
    for i, by in enumerate((1, -1)):

        @pl.when(side(i) & exists(PLANE * by))
        def _():
            list_copy(by).wait_recv()

    for turn in range(chunks + 3):
        if turn < chunks:
            near_stage(turn)
        if 0 <= turn - 1 < chunks:
            far_stage(turn - 1)
        if turn == 1:
            column_arrive(2)
            pass_text()
        if 0 <= turn - 2 < chunks:
            over_stage(turn - 2)
        if turn + AHEAD < chunks:
            near_start(turn + AHEAD)
        if 0 <= turn - 1 < chunks:
            first(turn - 1)
        if turn == 3:
            for m in range(1, PLANE):
                for j in range(2):
                    pass_copy(m, j).wait_recv()
        if 0 <= turn - 3:
            last_stage(turn - 3)
            second(turn - 3)

    w_copy.wait()
    wide = w.shape[1]
    parts = 4
    pw = wide // parts
    out_rows = rows // n_head

    def out_copy(d, p):
        peer = lax.rem(head + d, n_head)
        return pltpu.make_async_remote_copy(
            src_ref=partial.at[peer, :, pl.ds(p * pw, pw)],
            dst_ref=arrived.at[d - 1, :, pl.ds(p * pw, pw)],
            send_sem=out_send.at[d - 1, p],
            recv_sem=out_recv.at[d - 1, p],
            device_id={"head": peer},
            device_id_type=MESH,
        )

    for p in range(parts):
        for g in range(n_head):
            partial[g, :, pl.ds(p * pw, pw)] = jnp.dot(
                attended[pl.ds(g * out_rows, out_rows), :],
                w[:, pl.ds(p * pw, pw)],
                preferred_element_type=jnp.float32,
            ).astype(jnp.bfloat16)
        for d in range(1, n_head):
            out_copy(d, p).start()
    for p in range(parts):
        sums = partial[head, :, pl.ds(p * pw, pw)].astype(jnp.float32)
        for d in range(1, n_head):
            out_copy(d, p).wait_recv()
            sums = sums + arrived[d - 1, :, pl.ds(p * pw, pw)].astype(jnp.float32)
        out_ref[:, pl.ds(p * pw, pw)] = sums.astype(jnp.bfloat16)

    for i, by in enumerate((1, -1)):

        @pl.when(side(i) & exists(-PLANE * by))
        def _():
            list_copy(by).wait_send()

        @pl.when(jnp.logical_not(at_place(by, PLANE - 1)))
        def _():
            for c in range(chunks):
                for j in range(2):
                    near_copy(by, c, j).wait_send()

        @pl.when(at_place(by, PLANE - 2) & exists(2 * by))
        def _():
            for c in range(chunks):
                for j in range(2):
                    edge_copy(by, c, j).wait_send()

        @pl.when(side(i))
        def _():
            for c in range(chunks):
                for j in range(2):
                    far_copy(by, c, j).wait_send()

        @pl.when(side(i) & exists(PLANE * by))
        def _():
            for c in range(chunks):
                for j in range(2):
                    over_copy(by, c, j).wait_send()

        for step in range(1, PLANES_AROUND + 1):

            @pl.when(exists(PLANE * by) & exists(-PLANE * by * (step - 1)))
            def _():
                for j in range(2):
                    column_copy(by, step, j).wait_send()

    for m in range(1, PLANE):
        for j in range(2):
            pass_copy(m, j).wait_send()

    for p in range(parts):
        for d in range(1, n_head):
            out_copy(d, p).wait_send()


def body(n_seq, n_head, q, k, v, tk, tv, near, clip_lengths, text_lengths, w):
    rows, width = q.shape
    heads = width // HD
    group = GROUP if heads % GROUP == 0 else 1
    chunks = heads // group
    wide = w.shape[1]
    out_rows = rows // n_head
    trows = tk.shape[0]
    text_pad = -(-(COLUMN + 2 * (PLANE - 1)) * trows // 128) * 128
    padded = jnp.pad(near, ((0, 7), (0, 128 - near.shape[1])), constant_values=-1)
    smem = pl.BlockSpec(memory_space=pltpu.SMEM)
    hbm = pl.BlockSpec(memory_space=pl.ANY)
    dma = pltpu.SemaphoreType.DMA
    bf16, f32 = jnp.bfloat16, jnp.float32
    return pl.pallas_call(
        functools.partial(kernel, n_seq, n_head),
        out_shape=jax.ShapeDtypeStruct((out_rows, wide), bf16),
        in_specs=[smem] * 3 + [hbm] * 7,
        out_specs=pl.BlockSpec(memory_space=pltpu.VMEM),
        scratch_shapes=[
            pltpu.VMEM((rows, width), bf16),
            pltpu.VMEM((2, 5 * rows, width), bf16),
            pltpu.VMEM((2, text_pad, width), bf16),
            pltpu.VMEM((2, 2, rows, width), bf16),
            pltpu.VMEM(w.shape, bf16),
            pltpu.VMEM((rows, width), f32),
            pltpu.VMEM((rows, width), f32),
            pltpu.VMEM((rows, width), f32),
            pltpu.VMEM((rows, width), bf16),
            pltpu.VMEM((n_head, out_rows, wide), bf16),
            pltpu.VMEM((n_head - 1, out_rows, wide), bf16),
            pltpu.VMEM((2, 2 * (PLANE - 1) * trows, width), bf16),
            pltpu.VMEM((8, 128), jnp.int32),
            dma((2, chunks, 2)),
            dma((2, chunks, 2)),
            dma((2, chunks, 2)),
            dma((2, chunks, 2)),
            dma((2, chunks, 2)),
            dma((2, chunks, 2)),
            dma((2, PLANES_AROUND, 2)),
            dma((2, PLANES_AROUND, 2)),
            dma((PLANE - 1, 2)),
            dma((PLANE - 1, 2)),
            dma((2,)),
            dma((n_head - 1, 4)),
            dma((n_head - 1, 4)),
            dma((6,)),
        ],
        compiler_params=pltpu.CompilerParams(
            collective_id=0, has_side_effects=True, vmem_limit_bytes=58 << 20
        ),
    )(near, clip_lengths, text_lengths, q, k, v, tk, tv, w, padded)


def solution(mesh):
    placed = (
        P("seq", "head"),
        P("seq", "head"),
        P("seq", "head"),
        P("seq", "head"),
        P("seq", "head"),
        P("seq", None),
        P(),
        P(),
        P("head", None),
    )
    return jax.shard_map(
        functools.partial(body, mesh.shape["seq"], mesh.shape["head"]),
        mesh=mesh,
        in_specs=placed,
        out_specs=P(("seq", "head"), None),
        check_vma=False,
    )
```
